32 devices in a mesh: tm: 8 (over y, x, core), space: 4 (over z).
Axes of the slice: x: 2, y: 2, z: 4, core: 2. Of those that a mesh axis runs over, the one named last changes fastest.
Arguments:
- start_field: float32 [8, 64, 1024], P('tm', None, 'space'), may hold values from -6 to 6
- play_level: int32 [8, 64, 1024], P('tm', None, 'space'), may hold values from -8 to 8
- stiffness: float32 [4, 64, 64, 1024], P(None, None, None, 'space')
- columns: int32 [4, 1024], P(None, 'space'), may hold values from 0 to 287, as said below
- play_width: float32 [64, 1024], P(None, 'space'), may hold values from 0.05 to 0.5
- coil: float32 [3, 64, 1024], P(None, None, 'space'), may hold values from -6 to 6
- newton_counts: int32 [8, 4], P('tm'), may hold values from 1 to 3, as said below
Outputs:
- field_starts: float32 [8, 64, 1024], P('tm', None, 'space')
- play_starts: float32 [8, 64, 1024], P('tm', None, 'space')
The draws below stay inside these ranges and needn't reach their ends.
Inputs may be any that keep to these rules, and one draw needn't show every extreme that they name: `columns`: slot 0 is the block itself, 16 plus its local index; every slot lies within 16 of that, counting the partition's blocks extended by 16 interface blocks on each side. `newton_counts`: the same for all partitions of a slice.
All inputs are finite; a program needn't handle non-finite values.
Results may differ from the reference program's by a relative error of at most 0.00016.
Values sent between devices are 32-bit elements; how exact they have to be, the bound alone decides.
A program may use at most 64 MiB of HBM per device.

```python
import math
import jax
import jax.numpy as jnp
from jax import lax

BLK = 64
NNZ = 4
NBLK = 256
NIF = 16
STEPS = 4
NEWT = 3
ITERS = 2
SLICES = 8
NCOL = 1024


def draw_stiffness(key, part):
    key_diag, key_off = jax.random.split(key)
    diag_vals = jax.random.uniform(key_diag, (BLK, NCOL), jnp.float32, 2.0, 4.0)
    off = 0.015 * jax.random.normal(key_off, (NNZ, BLK, BLK, NCOL), jnp.float32)
    eye_block = jnp.eye(BLK, dtype=jnp.float32)[:, :, None]
    first = off[0] * (1.0 - eye_block) + eye_block * diag_vals[None, :, :]
    return jnp.concatenate([first[None], off[1:]], axis=0)


def draw_columns(key, part):
    local = jnp.arange(NCOL, dtype=jnp.int32) % NBLK
    shifts = jax.random.randint(key, (NNZ - 1, NCOL), -NIF, NIF + 1, dtype=jnp.int32)
    first_row = jnp.where(local == 0, -NIF, jnp.where(local == NBLK - 1, NIF, shifts[0]))
    shifts = jnp.concatenate([jnp.zeros((1, NCOL), jnp.int32), first_row[None], shifts[1:]], axis=0)
    return (local[None, :] + NIF + shifts).astype(jnp.int32)


def draw_newton_counts(key, part):
    key_vals, key_top, key_low = jax.random.split(key, 3)
    total = SLICES * STEPS
    flat = jax.random.randint(key_vals, (total,), 1, NEWT + 1, dtype=jnp.int32)
    top_at = jax.random.randint(key_top, (), 0, total, dtype=jnp.int32)
    low_at = (top_at + 1 + jax.random.randint(key_low, (), 0, total - 1, dtype=jnp.int32)) % total
    spots = jnp.arange(total, dtype=jnp.int32)
    flat = jnp.where(spots == top_at, NEWT, jnp.where(spots == low_at, 1, flat))
    return flat.reshape(SLICES, STEPS)


def set_ends(result, own_key, least, top_value):
    spot = [jax.random.randint(jax.random.fold_in(own_key, axis), (), 0, length) for axis, length in enumerate(result.shape)]
    longest = result.shape.index(max(result.shape))
    beside = spot[:longest] + [(spot[longest] + 1) % result.shape[longest]] + spot[longest + 1:]
    return result.at[tuple(spot)].set(least).at[tuple(beside)].set(top_value)


def shard_levels(rng, dims, shards, smallest, high):
    gain, own = 1.0, jax.random.fold_in(rng, 6)
    for dim, blocks in shards:
        heights = jnp.exp(jax.random.uniform(jax.random.fold_in(own, dim), (blocks,), jnp.float32, smallest / len(shards), high / len(shards)))
        gain = gain * jnp.repeat(heights, dims[dim] // blocks).reshape([-1 if axis == dim else 1 for axis in range(len(dims))])
    return gain


def gaussian(own_key, shape, width, reach, cuts=(), kind=jnp.bfloat16):
    values = width * jax.random.normal(own_key, shape, jnp.float32)
    if cuts:
        values = values * shard_levels(own_key, shape, cuts, -0.22, 0.18)
    return jnp.clip(values, -reach, reach).astype(kind)


def setup_inputs(seed: int = 0) -> dict:
    seeds = jax.random.split(jax.random.key(seed), 8)
    return {
        "start_field": gaussian(seeds[0], (SLICES, BLK, NCOL), 1.0, 6.0, ((0, 8), (2, 4)), jnp.float32),
        "play_level": set_ends(jax.random.randint(seeds[1], (SLICES, BLK, NCOL), -8, 9), jax.random.fold_in(seeds[1], 1), -8, 8).astype(jnp.int32),
        "stiffness": draw_stiffness(jax.random.fold_in(seeds[7], 71), 0),
        "columns": draw_columns(jax.random.fold_in(seeds[7], 71), 0),
        "play_width": jnp.clip(jnp.exp(math.log(0.5) - 2.3025851 * jax.random.uniform(seeds[4], (BLK, NCOL), jnp.float32) ** shard_levels(seeds[4], (BLK, NCOL), ((1, 4),), -0.2, 0.2)), 0.05, 0.5),
        "coil": gaussian(seeds[5], (3, BLK, NCOL), 1.0, 6.0, ((2, 4),), jnp.float32),
        "newton_counts": draw_newton_counts(jax.random.fold_in(seeds[7], 71), 0),
    }


tau_step = 0.5
play_gain = 1.0
play_quantum = 0.05


def reference(start_field, play_level, stiffness, columns, play_width, coil, newton_counts):
    picks = jnp.arange(BLK, dtype=jnp.int32)
    diag_entries = stiffness[0][picks, picks, :]
    jacobi = 1.0 + tau_step * (diag_entries + play_gain)
    damping = 1.0 / jacobi
    offsets = (jnp.arange(NCOL, dtype=jnp.int32) // NBLK) * NBLK
    global_cols = (offsets[None, :] + columns).astype(jnp.int32)
    phases = jnp.arange(3, dtype=jnp.float32) * (2.0 * math.pi / 3.0)

    def apply_stiffness(field):
        padded = jnp.pad(field, ((0, 0), (0, 0), (NIF, NIF)))
        picked = padded[:, :, global_cols]
        return jnp.einsum("sabj,gbsj->gaj", stiffness, picked, precision=lax.Precision.HIGHEST)

    def fine(field, play_state):
        for step in range(STEPS):
            moment = (jnp.arange(SLICES, dtype=jnp.float32) * STEPS + (step + 1)) * (2.0 * math.pi / (SLICES * STEPS))
            waves = jnp.sin(moment[:, None] + phases[None, :])
            source = waves[:, 0, None, None] * coil[0] + waves[:, 1, None, None] * coil[1] + waves[:, 2, None, None] * coil[2]
            counts = newton_counts[:, step][:, None, None]
            guess = field
            for counter in range(NEWT):
                bound = jnp.minimum(jnp.maximum(play_state, guess - play_width), guess + play_width)
                resid = guess - field - tau_step * (source - apply_stiffness(guess) - play_gain * bound)
                guess = jnp.where(counter < counts, guess - resid / jacobi, guess)
            play_state = jnp.minimum(jnp.maximum(play_state, guess - play_width), guess + play_width)
            field = guess
        return field, play_state

    field = start_field
    play_state = play_level.astype(jnp.float32) * play_quantum
    for rounds in range(ITERS):
        fine_a, fine_p = fine(field, play_state)
        extra_a = fine_a - damping * field
        extra_p = fine_p - play_state
        new_a = [fine_a[SLICES - 1]]
        new_p = [fine_p[SLICES - 1]]
        for slot in range(SLICES - 1):
            new_a.append(damping * new_a[-1] + extra_a[slot])
            new_p.append(new_p[-1] + extra_p[slot])
        field = jnp.stack(new_a)
        play_state = jnp.stack(new_p)
    return field, play_state
```

```python
import functools
import math

import jax
import jax.numpy as jnp
from jax import lax
from jax.experimental import pallas as pl
from jax.experimental.pallas import tpu as pltpu
from jax.sharding import PartitionSpec as P

NIF = 16
NEWT = 3
ITERS = 2
ROWS = 8
LANES = 128

tau_step = 0.5
play_gain = 1.0
play_quantum = 0.05

MESH = pl.DeviceIdType.MESH


def merge_rows(sums):
    row = lax.broadcasted_iota(jnp.int32, (ROWS, LANES), 0)
    width = 1
    while len(sums) > 1:
        low = (row & width) == 0
        sums = [
            jnp.where(low, even, odd) + pltpu.roll(jnp.where(low, odd, even), width, 0)
            for even, odd in zip(sums[::2], sums[1::2])
        ]
        width *= 2
    return sums[0]


def play(state, guess, width):
    return jnp.minimum(jnp.maximum(state, guess - width), guess + width)


def kernel(
    slices, parts, strides,
    start_ref, level_ref, stiff_hbm, columns_ref, width_ref, coil_ref, counts_ref,
    out_ref,
    stiff, guess, field, state, damp, first, picked, source, index, inside,
    edge_out, edge_in, own, mixed, arrived,
    stiff_sem, edge_send, edge_recv, scan_send, scan_recv,
):
    nnz, blk, _, local = stiff.shape
    groups, tiles = blk // ROWS, local // LANES
    steps = counts_ref.shape[1]
    slice_index = lax.axis_index("tm")
    part = lax.axis_index("space")
    has_left, has_right = part > 0, part < parts - 1

    loads = [
        pltpu.make_async_copy(stiff_hbm.at[s], stiff.at[s], stiff_sem.at[s]) for s in range(nnz)
    ]
    for load in loads:
        load.start()

    edge_in[...] = jnp.zeros_like(edge_in)
    offsets = sorted({d % slices for d in strides} | {-d % slices for d in strides})
    barrier = pltpu.get_barrier_semaphore()
    for offset in offsets:
        pl.semaphore_signal(
            barrier, inc=1, device_id={"tm": lax.rem(slice_index + offset, slices)},
            device_id_type=MESH,
        )

    @pl.when(has_left)
    def _():
        pl.semaphore_signal(barrier, inc=1, device_id={"space": part - 1}, device_id_type=MESH)

    @pl.when(has_right)
    def _():
        pl.semaphore_signal(barrier, inc=1, device_id={"space": part + 1}, device_id_type=MESH)

    lane = lax.broadcasted_iota(jnp.int32, (ROWS, LANES), 1)
    row = lax.broadcasted_iota(jnp.int32, (ROWS, LANES), 0)
    group_of_lane = lane // NIF

    def rows(g):
        return pl.ds(g * ROWS if isinstance(g, int) else pl.multiple_of(g * ROWS, ROWS), ROWS)

    def tile(t):
        return pl.ds(t * LANES, LANES)

    for s in range(1, nnz):
        for t in range(tiles):
            place = columns_ref[s : s + 1, t * LANES : (t + 1) * LANES] - (NIF + t * LANES)
            place = jnp.broadcast_to(place, (ROWS, LANES))
            index[s - 1, t] = place & (LANES - 1)
            inside[s - 1, t] = jnp.where((place >= 0) & (place < LANES), 1, 0)

    for step in range(steps):
        moment = (slice_index.astype(jnp.float32) * steps + (step + 1)) * (
            2.0 * math.pi / (slices * steps)
        )
        waves = [
            jnp.sin(jnp.full((ROWS, LANES), moment + h * (2.0 * math.pi / 3.0), jnp.float32))
            for h in range(3)
        ]
        for g in range(groups):
            for t in range(tiles):
                here = (rows(g), tile(t))
                source[(step, *here)] = (
                    waves[0] * coil_ref[(0, *here)]
                    + waves[1] * coil_ref[(1, *here)]
                    + waves[2] * coil_ref[(2, *here)]
                )

    field[...] = start_ref[0]
    guess[...] = start_ref[0]
    state[0] = level_ref[0].astype(jnp.float32) * play_quantum
    state[1] = level_ref[0].astype(jnp.float32) * play_quantum

    loads[0].wait()
    for g in range(groups):
        for t in range(tiles):
            diag = jnp.zeros((ROWS, LANES), jnp.float32)
            for r in range(ROWS):
                diag = jnp.where(row == r, stiff[0, g * ROWS + r, rows(g), tile(t)], diag)
            damp[rows(g), tile(t)] = 1.0 / (1.0 + tau_step * (diag + play_gain))

    pl.semaphore_wait(
        barrier, len(offsets) + has_left.astype(jnp.int32) + has_right.astype(jnp.int32)
    )

    def products(slots, g, t):
        sums = [None] * ROWS
        for s in slots:
            for b in range(groups):
                vector = guess[rows(b), tile(t)] if s == 0 else picked[s - 1, rows(b), tile(t)]
                for r in range(ROWS):
                    term = stiff[s, g * ROWS + r, rows(b), tile(t)] * vector
                    sums[r] = term if sums[r] is None else sums[r] + term
        return merge_rows(sums)

    def sweep(step, counter, begin):
        slot = lax.rem(step * NEWT + counter, 2)
        upper = lower = None
        for b in range(groups):
            last = guess[rows(b), tile(tiles - 1)]
            head = guess[rows(b), tile(0)]
            if b == 0:
                upper, lower = last, head
            else:
                upper = jnp.where(
                    group_of_lane == LANES // NIF - 1 - b,
                    pltpu.roll(last, LANES - NIF * b, 1), upper,
                )
                lower = jnp.where(group_of_lane == b, pltpu.roll(head, NIF * b, 1), lower)
        edge_out[0] = upper
        edge_out[1] = lower
        up = pltpu.make_async_remote_copy(
            src_ref=edge_out.at[0], dst_ref=edge_in.at[0, slot],
            send_sem=edge_send.at[0], recv_sem=edge_recv.at[0, slot],
            device_id={"space": part + 1}, device_id_type=MESH,
        )
        down = pltpu.make_async_remote_copy(
            src_ref=edge_out.at[1], dst_ref=edge_in.at[1, slot],
            send_sem=edge_send.at[1], recv_sem=edge_recv.at[1, slot],
            device_id={"space": part - 1}, device_id_type=MESH,
        )

        @pl.when(has_right)
        def _():
            up.start()

        @pl.when(has_left)
        def _():
            down.start()

        @pl.loop(0, groups)
        def _(g):
            for t in range(tiles):
                first[rows(g), tile(t)] = products((0,), g, t)

        begin(counter)

        @pl.when(has_right)
        def _():
            up.wait_send()
            down.wait_recv()

        @pl.when(has_left)
        def _():
            down.wait_send()
            up.wait_recv()

        left_edge, right_edge = edge_in[0, slot], edge_in[1, slot]
        for b in range(groups):
            blocks = [guess[rows(b), tile(t)] for t in range(tiles)]
            before = left_edge if b == 0 else pltpu.roll(left_edge, NIF * b, 1)
            after = right_edge if b == 0 else pltpu.roll(right_edge, LANES - NIF * b, 1)
            chain = [before, *blocks, after]
            for t in range(tiles):
                beside = jnp.where(lane < LANES // 2, chain[t + 2], chain[t])
                for s in range(1, nnz):
                    where = index[s - 1, t]
                    picked[s - 1, rows(b), tile(t)] = jnp.where(
                        inside[s - 1, t] == 1,
                        jnp.take_along_axis(blocks[t], where, axis=1, mode="promise_in_bounds"),
                        jnp.take_along_axis(beside, where, axis=1, mode="promise_in_bounds"),
                    )

        active = jnp.full((ROWS, LANES), counter, jnp.int32) < jnp.full(
            (ROWS, LANES), counts_ref[0, step], jnp.int32
        )

        @pl.loop(0, groups)
        def _(g):
            for t in range(tiles):
                here = (rows(g), tile(t))
                applied = first[here] + products(range(1, nnz), g, t)
                x = guess[here]
                bound = play(state[(0, *here)], x, width_ref[here])
                resid = x - field[here] - tau_step * (
                    source[(step, *here)] - applied - play_gain * bound
                )
                guess[here] = jnp.where(active, x - resid * damp[here], x)

    def wait_stiffness(counter):
        @pl.when(counter == 0)
        def _():
            for load in loads[1:]:
                load.wait()

    for round_ in range(ITERS):

        @pl.loop(0, steps)
        def _(step):
            @pl.loop(0, NEWT)
            def _(counter):
                if round_ == 0:
                    sweep(step, counter, lambda c: wait_stiffness(step * NEWT + c))
                else:
                    sweep(step, counter, lambda c: None)

            state[0] = play(state[0], guess[...], width_ref[...])
            field[...] = guess[...]

        begin_a = start_ref[0] if round_ == 0 else out_ref[0, 0]
        fine_a, fine_p = guess[...], state[0]
        full = jnp.full((blk, local), slice_index, jnp.int32) == slices - 1
        own[round_, 0] = jnp.where(full, fine_a, fine_a - damp[...] * begin_a)
        own[round_, 1] = jnp.where(full, fine_p, fine_p - state[1])

        def send(source_ref, place, distance):
            return pltpu.make_async_remote_copy(
                src_ref=source_ref, dst_ref=arrived.at[round_, place],
                send_sem=scan_send.at[round_, place], recv_sem=scan_recv.at[round_, place],
                device_id={"tm": lax.rem(slice_index + distance, slices)},
                device_id_type=MESH,
            )

        near = send(own.at[round_], 0, 1)
        near.start()
        far = send(own.at[round_], 1, 2)

        @pl.when(slice_index != slices - 2)
        def _():
            far.start()

        near.wait_recv()
        mixed[round_, 0] = arrived[round_, 0]

        @pl.when(slice_index != 0)
        def _():
            far.wait_recv()
            mixed[round_, 0, 0] = arrived[round_, 0, 0] + damp[...] * arrived[round_, 1, 0]
            mixed[round_, 0, 1] = arrived[round_, 0, 1] + arrived[round_, 1, 1]

        near.wait_send()

        @pl.when(slice_index != slices - 2)
        def _():
            far.wait_send()

        power = damp[...]
        stage, distance = 0, 2
        while distance < slices:
            power = power * power
            hop = send(mixed.at[round_, stage], stage + 2, distance)

            @pl.when(slice_index + distance < slices)
            def _():
                hop.start()

            mixed[round_, stage + 1] = mixed[round_, stage]

            @pl.when(slice_index >= distance)
            def _():
                hop.wait_recv()
                mixed[round_, stage + 1, 0] = (
                    mixed[round_, stage, 0] + power * arrived[round_, stage + 2, 0]
                )
                mixed[round_, stage + 1, 1] = (
                    mixed[round_, stage, 1] + arrived[round_, stage + 2, 1]
                )

            @pl.when(slice_index + distance < slices)
            def _():
                hop.wait_send()

            stage, distance = stage + 1, distance * 2

        out_ref[0, 0] = mixed[round_, stage, 0]
        out_ref[1, 0] = mixed[round_, stage, 1]
        if round_ < ITERS - 1:
            guess[...] = mixed[round_, stage, 0]
            field[...] = mixed[round_, stage, 0]
            state[0] = mixed[round_, stage, 1]
            state[1] = mixed[round_, stage, 1]


def on_device(start_field, play_level, stiffness, columns, play_width, coil, newton_counts):
    slices, parts = lax.axis_size("tm"), lax.axis_size("space")
    nnz, blk, _, local = stiffness.shape
    strides = [1, 2]
    while strides[-1] * 2 < slices:
        strides.append(strides[-1] * 2)
    stages = len(strides) - 1
    tiles, groups, steps = local // LANES, blk // ROWS, newton_counts.shape[1]
    vmem = pl.BlockSpec(memory_space=pltpu.VMEM)
    plane = (blk, local)
    f32 = jnp.float32
    both = pl.pallas_call(
        functools.partial(kernel, slices, parts, strides),
        out_shape=jax.ShapeDtypeStruct((2, 1, *plane), f32),
        in_specs=[
            vmem, vmem, pl.BlockSpec(memory_space=pl.ANY), vmem, vmem, vmem,
            pl.BlockSpec(memory_space=pltpu.SMEM),
        ],
        out_specs=vmem,
        scratch_shapes=[
            pltpu.VMEM(stiffness.shape, f32),
            pltpu.VMEM(plane, f32),
            pltpu.VMEM(plane, f32),
            pltpu.VMEM((2, *plane), f32),
            pltpu.VMEM(plane, f32),
            pltpu.VMEM(plane, f32),
            pltpu.VMEM((nnz - 1, *plane), f32),
            pltpu.VMEM((steps, *plane), f32),
            pltpu.VMEM((nnz - 1, tiles, ROWS, LANES), jnp.int32),
            pltpu.VMEM((nnz - 1, tiles, ROWS, LANES), jnp.int32),
            pltpu.VMEM((2, ROWS, LANES), f32),
            pltpu.VMEM((2, 2, ROWS, LANES), f32),
            pltpu.VMEM((ITERS, 2, *plane), f32),
            pltpu.VMEM((ITERS, stages + 1, 2, *plane), f32),
            pltpu.VMEM((ITERS, stages + 2, 2, *plane), f32),
            pltpu.SemaphoreType.DMA((nnz,)),
            pltpu.SemaphoreType.DMA((2,)),
            pltpu.SemaphoreType.DMA((2, 2)),
            pltpu.SemaphoreType.DMA((ITERS, stages + 2)),
            pltpu.SemaphoreType.DMA((ITERS, stages + 2)),
        ],
        compiler_params=pltpu.CompilerParams(
            collective_id=0, has_side_effects=True, vmem_limit_bytes=48 * 1024 * 1024
        ),
        name="parareal",
    )(start_field, play_level, stiffness, columns, play_width, coil, newton_counts)
    return both[0], both[1]


def solution(mesh):
    return jax.shard_map(
        on_device,
        mesh=mesh,
        in_specs=(
            P("tm", None, "space"),
            P("tm", None, "space"),
            P(None, None, None, "space"),
            P(None, "space"),
            P(None, "space"),
            P(None, None, "space"),
            P("tm", None),
        ),
        out_specs=(P("tm", None, "space"), P("tm", None, "space")),
        check_vma=False,
    )
```

```python
import functools
import math

import jax
import jax.numpy as jnp
from jax import lax
from jax.experimental import pallas as pl
from jax.experimental.pallas import tpu as pltpu
from jax.sharding import PartitionSpec as P

NIF = 16
NEWT = 3
ITERS = 2
ROWS = 8
LANES = 128

tau_step = 0.5
play_gain = 1.0
play_quantum = 0.05

MESH = pl.DeviceIdType.MESH


def merge_rows(sums):
    row = lax.broadcasted_iota(jnp.int32, (ROWS, LANES), 0)
    width = 1
    while len(sums) > 1:
        low = (row & width) == 0
        sums = [
            jnp.where(low, even, odd) + pltpu.roll(jnp.where(low, odd, even), width, 0)
            for even, odd in zip(sums[::2], sums[1::2])
        ]
        width *= 2
    return sums[0]


def play(state, guess, width):
    return jnp.minimum(jnp.maximum(state, guess - width), guess + width)


def kernel(
    slices, parts, strides,
    start_hbm, level_hbm, stiff_hbm, columns_hbm, width_hbm, coil_hbm, counts_ref,
    out_ref,
    start_ref, level_ref, columns_ref, width_ref, coil_ref, small_sem,
    stiff, guess, field, state, damp, first, picked, source, index, inside,
    edge_stiff, edge_picked, edge_index, edge_valid,
    edge_out, edge_in, own, mixed, arrived,
    stiff_sem, edge_send, edge_recv, scan_send, scan_recv,
):
    nnz, blk, _, local = stiff.shape
    groups, tiles = blk // ROWS, local // LANES
    steps = counts_ref.shape[1]
    slice_index = lax.axis_index("tm")
    part = lax.axis_index("space")
    has_left, has_right = part > 0, part < parts - 1

    small = [
        pltpu.make_async_copy(source_, target, small_sem.at[k])
        for k, (source_, target) in enumerate((
            (columns_hbm, columns_ref), (coil_hbm, coil_ref), (start_hbm, start_ref),
            (level_hbm, level_ref), (width_hbm, width_ref),
        ))
    ]
    for load in small:
        load.start()
    loads = [
        pltpu.make_async_copy(stiff_hbm.at[s], stiff.at[s], stiff_sem.at[s]) for s in range(nnz)
    ]
    for load in loads:
        load.start()

    edge_in[...] = jnp.zeros_like(edge_in)
    offsets = sorted({d % slices for d in strides} | {-d % slices for d in strides})
    barrier = pltpu.get_barrier_semaphore()
    for offset in offsets:
        pl.semaphore_signal(
            barrier, inc=1, device_id={"tm": lax.rem(slice_index + offset, slices)},
            device_id_type=MESH,
        )

    @pl.when(has_left)
    def _():
        pl.semaphore_signal(barrier, inc=1, device_id={"space": part - 1}, device_id_type=MESH)

    @pl.when(has_right)
    def _():
        pl.semaphore_signal(barrier, inc=1, device_id={"space": part + 1}, device_id_type=MESH)

    lane = lax.broadcasted_iota(jnp.int32, (ROWS, LANES), 1)
    row = lax.broadcasted_iota(jnp.int32, (ROWS, LANES), 0)
    group_of_lane = lane // NIF

    def take(values, where):
        return jnp.take_along_axis(values, where, axis=1, mode="promise_in_bounds")

    def rows(g):
        return pl.ds(g * ROWS if isinstance(g, int) else pl.multiple_of(g * ROWS, ROWS), ROWS)

    def tile(t):
        return pl.ds(t * LANES, LANES)

    for load in small:
        load.wait()
    for s in range(1, nnz):
        for t in range(tiles):
            place = columns_ref[s : s + 1, t * LANES : (t + 1) * LANES] - (NIF + t * LANES)
            place = jnp.broadcast_to(place, (ROWS, LANES))
            index[s - 1, t] = place & (LANES - 1)
            inside[s - 1, t] = jnp.where((place >= 0) & (place < LANES), 1, 0)
            if t == 0:
                near = take(place, lane & (NIF - 1))
                edge_index[0, s - 1] = group_of_lane * NIF + (near & (NIF - 1))
                edge_valid[0, s - 1] = jnp.where(near < 0, 1.0, 0.0)
            if t == tiles - 1:
                near = take(place, LANES - NIF + (lane & (NIF - 1)))
                edge_index[1, s - 1] = group_of_lane * NIF + (near & (NIF - 1))
                edge_valid[1, s - 1] = jnp.where(near >= LANES, 1.0, 0.0)

    for step in range(steps):
        moment = (slice_index.astype(jnp.float32) * steps + (step + 1)) * (
            2.0 * math.pi / (slices * steps)
        )
        waves = [
            jnp.sin(jnp.full((ROWS, LANES), moment + h * (2.0 * math.pi / 3.0), jnp.float32))
            for h in range(3)
        ]
        for g in range(groups):
            for t in range(tiles):
                here = (rows(g), tile(t))
                source[(step, *here)] = (
                    waves[0] * coil_ref[(0, *here)]
                    + waves[1] * coil_ref[(1, *here)]
                    + waves[2] * coil_ref[(2, *here)]
                )

    field[...] = start_ref[0]
    guess[...] = start_ref[0]
    state[0] = level_ref[0].astype(jnp.float32) * play_quantum
    state[1] = level_ref[0].astype(jnp.float32) * play_quantum

    loads[0].wait()
    for g in range(groups):
        for t in range(tiles):
            diag = jnp.zeros((ROWS, LANES), jnp.float32)
            for r in range(ROWS):
                diag = jnp.where(row == r, stiff[0, g * ROWS + r, rows(g), tile(t)], diag)
            damp[rows(g), tile(t)] = 1.0 / (1.0 + tau_step * (diag + play_gain))

    pl.semaphore_wait(
        barrier, len(offsets) + has_left.astype(jnp.int32) + has_right.astype(jnp.int32)
    )

    for s in range(1, nnz):
        loads[s].wait()

        @pl.loop(0, blk, unroll=8)
        def _(a):
            left = right = None
            for b in range(groups):
                head = stiff[s, a, rows(b), tile(0)]
                last = stiff[s, a, rows(b), tile(tiles - 1)]
                q = LANES // NIF - 1 - b
                head = head if q == 0 else pltpu.roll(head, NIF * q, 1)
                shift = (NIF * b + NIF) % LANES
                last = last if shift == 0 else pltpu.roll(last, shift, 1)
                left = head if b == 0 else jnp.where(group_of_lane == q, head, left)
                right = last if b == 0 else jnp.where(group_of_lane == b, last, right)
            edge_stiff[0, s - 1, a] = jnp.where(edge_valid[0, s - 1] == 1.0, left, 0.0)
            edge_stiff[1, s - 1, a] = jnp.where(edge_valid[1, s - 1] == 1.0, right, 0.0)

    def products(slots, g, t):
        sums = [None] * ROWS
        for s in slots:
            for b in range(groups):
                vector = guess[rows(b), tile(t)] if s == 0 else picked[s - 1, rows(b), tile(t)]
                for r in range(ROWS):
                    term = stiff[s, g * ROWS + r, rows(b), tile(t)] * vector
                    sums[r] = term if sums[r] is None else sums[r] + term
        return merge_rows(sums)

    def sweep(step, counter):
        slot = lax.rem(step * NEWT + counter, 2)
        upper = lower = None
        for b in range(groups):
            last = guess[rows(b), tile(tiles - 1)]
            head = guess[rows(b), tile(0)]
            if b == 0:
                upper, lower = last, head
            else:
                upper = jnp.where(
                    group_of_lane == LANES // NIF - 1 - b,
                    pltpu.roll(last, LANES - NIF * b, 1), upper,
                )
                lower = jnp.where(group_of_lane == b, pltpu.roll(head, NIF * b, 1), lower)
        edge_out[0] = upper
        edge_out[1] = lower
        up = pltpu.make_async_remote_copy(
            src_ref=edge_out.at[0], dst_ref=edge_in.at[0, slot],
            send_sem=edge_send.at[0], recv_sem=edge_recv.at[0, slot],
            device_id={"space": part + 1}, device_id_type=MESH,
        )
        down = pltpu.make_async_remote_copy(
            src_ref=edge_out.at[1], dst_ref=edge_in.at[1, slot],
            send_sem=edge_send.at[1], recv_sem=edge_recv.at[1, slot],
            device_id={"space": part - 1}, device_id_type=MESH,
        )

        @pl.when(has_right)
        def _():
            up.start()

        @pl.when(has_left)
        def _():
            down.start()

        nothing = jnp.zeros((ROWS, LANES), jnp.float32)
        for b in range(groups):
            blocks = [guess[rows(b), tile(t)] for t in range(tiles)]
            chain = [nothing, *blocks, nothing]
            for t in range(tiles):
                beside = jnp.where(lane < LANES // 2, chain[t + 2], chain[t])
                for s in range(1, nnz):
                    where = index[s - 1, t]
                    picked[s - 1, rows(b), tile(t)] = jnp.where(
                        inside[s - 1, t] == 1, take(blocks[t], where), take(beside, where)
                    )

        @pl.loop(0, groups)
        def _(g):
            for t in range(tiles):
                first[rows(g), tile(t)] = products(range(nnz), g, t)

        @pl.when(has_right)
        def _():
            up.wait_send()
            down.wait_recv()

        @pl.when(has_left)
        def _():
            down.wait_send()
            up.wait_recv()

        for side in range(2):
            edge = edge_in[side, slot]
            for s in range(1, nnz):
                edge_picked[side, s - 1] = take(edge, edge_index[side, s - 1])

        active = jnp.full((ROWS, LANES), counter, jnp.int32) < jnp.full(
            (ROWS, LANES), counts_ref[0, step], jnp.int32
        )

        def edge_products(side, g):
            total = merge_rows([
                sum(
                    edge_stiff[side, s, g * ROWS + r] * edge_picked[side, s]
                    for s in range(nnz - 1)
                )
                for r in range(ROWS)
            ])
            width = LANES // 2
            while width >= NIF:
                total = total + pltpu.roll(total, width, 1)
                width //= 2
            at_edge = lane < NIF if side == 0 else lane >= LANES - NIF
            return jnp.where(at_edge, total, 0.0)

        for g in range(groups):
            for t in range(tiles):
                here = (rows(g), tile(t))
                applied = first[here]
                if t == 0:
                    applied = applied + edge_products(0, g)
                if t == tiles - 1:
                    applied = applied + edge_products(1, g)
                x = guess[here]
                bound = play(state[(0, *here)], x, width_ref[here])
                resid = x - field[here] - tau_step * (
                    source[(step, *here)] - applied - play_gain * bound
                )
                guess[here] = jnp.where(active, x - resid * damp[here], x)

    for round_ in range(ITERS):

        @pl.loop(0, steps)
        def _(step):
            @pl.loop(0, NEWT)
            def _(counter):
                sweep(step, counter)

            state[0] = play(state[0], guess[...], width_ref[...])
            field[...] = guess[...]

        begin_a = start_ref[0] if round_ == 0 else out_ref[0, 0]
        fine_a, fine_p = guess[...], state[0]
        full = jnp.full((blk, local), slice_index, jnp.int32) == slices - 1
        own[round_, 0] = jnp.where(full, fine_a, fine_a - damp[...] * begin_a)
        own[round_, 1] = jnp.where(full, fine_p, fine_p - state[1])

        def send(source_ref, place, distance):
            return pltpu.make_async_remote_copy(
                src_ref=source_ref, dst_ref=arrived.at[round_, place],
                send_sem=scan_send.at[round_, place], recv_sem=scan_recv.at[round_, place],
                device_id={"tm": lax.rem(slice_index + distance, slices)},
                device_id_type=MESH,
            )

        near = send(own.at[round_], 0, 1)
        near.start()
        far = send(own.at[round_], 1, 2)

        @pl.when(slice_index != slices - 2)
        def _():
            far.start()

        near.wait_recv()
        mixed[round_, 0] = arrived[round_, 0]

        @pl.when(slice_index != 0)
        def _():
            far.wait_recv()
            mixed[round_, 0, 0] = arrived[round_, 0, 0] + damp[...] * arrived[round_, 1, 0]
            mixed[round_, 0, 1] = arrived[round_, 0, 1] + arrived[round_, 1, 1]

        near.wait_send()

        @pl.when(slice_index != slices - 2)
        def _():
            far.wait_send()

        power = damp[...]
        stage, distance = 0, 2
        while distance < slices:
            power = power * power
            hop = send(mixed.at[round_, stage], stage + 2, distance)

            @pl.when(slice_index + distance < slices)
            def _():
                hop.start()

            mixed[round_, stage + 1] = mixed[round_, stage]

            @pl.when(slice_index >= distance)
            def _():
                hop.wait_recv()
                mixed[round_, stage + 1, 0] = (
                    mixed[round_, stage, 0] + power * arrived[round_, stage + 2, 0]
                )
                mixed[round_, stage + 1, 1] = (
                    mixed[round_, stage, 1] + arrived[round_, stage + 2, 1]
                )

            @pl.when(slice_index + distance < slices)
            def _():
                hop.wait_send()

            stage, distance = stage + 1, distance * 2

        out_ref[0, 0] = mixed[round_, stage, 0]
        out_ref[1, 0] = mixed[round_, stage, 1]
        if round_ < ITERS - 1:
            guess[...] = mixed[round_, stage, 0]
            field[...] = mixed[round_, stage, 0]
            state[0] = mixed[round_, stage, 1]
            state[1] = mixed[round_, stage, 1]


def on_device(start_field, play_level, stiffness, columns, play_width, coil, newton_counts):
    slices, parts = lax.axis_size("tm"), lax.axis_size("space")
    nnz, blk, _, local = stiffness.shape
    strides = [1, 2]
    while strides[-1] * 2 < slices:
        strides.append(strides[-1] * 2)
    stages = len(strides) - 1
    tiles, groups, steps = local // LANES, blk // ROWS, newton_counts.shape[1]
    vmem = pl.BlockSpec(memory_space=pltpu.VMEM)
    plane = (blk, local)
    f32 = jnp.float32
    both = pl.pallas_call(
        functools.partial(kernel, slices, parts, strides),
        out_shape=jax.ShapeDtypeStruct((2, 1, *plane), f32),
        in_specs=[
            *[pl.BlockSpec(memory_space=pltpu.HBM)] * 6,
            pl.BlockSpec(memory_space=pltpu.SMEM),
        ],
        out_specs=vmem,
        scratch_shapes=[
            pltpu.VMEM(start_field.shape, f32),
            pltpu.VMEM(play_level.shape, jnp.int32),
            pltpu.VMEM(columns.shape, jnp.int32),
            pltpu.VMEM(plane, f32),
            pltpu.VMEM(coil.shape, f32),
            pltpu.SemaphoreType.DMA((5,)),
            pltpu.VMEM(stiffness.shape, f32),
            pltpu.VMEM(plane, f32),
            pltpu.VMEM(plane, f32),
            pltpu.VMEM((2, *plane), f32),
            pltpu.VMEM(plane, f32),
            pltpu.VMEM(plane, f32),
            pltpu.VMEM((nnz - 1, *plane), f32),
            pltpu.VMEM((steps, *plane), f32),
            pltpu.VMEM((nnz - 1, tiles, ROWS, LANES), jnp.int32),
            pltpu.VMEM((nnz - 1, tiles, ROWS, LANES), jnp.int32),
            pltpu.VMEM((2, nnz - 1, blk, ROWS, LANES), f32),
            pltpu.VMEM((2, nnz - 1, ROWS, LANES), f32),
            pltpu.VMEM((2, nnz - 1, ROWS, LANES), jnp.int32),
            pltpu.VMEM((2, nnz - 1, ROWS, LANES), f32),
            pltpu.VMEM((2, ROWS, LANES), f32),
            pltpu.VMEM((2, 2, ROWS, LANES), f32),
            pltpu.VMEM((ITERS, 2, *plane), f32),
            pltpu.VMEM((ITERS, stages + 1, 2, *plane), f32),
            pltpu.VMEM((ITERS, stages + 2, 2, *plane), f32),
            pltpu.SemaphoreType.DMA((nnz,)),
            pltpu.SemaphoreType.DMA((2,)),
            pltpu.SemaphoreType.DMA((2, 2)),
            pltpu.SemaphoreType.DMA((ITERS, stages + 2)),
            pltpu.SemaphoreType.DMA((ITERS, stages + 2)),
        ],
        compiler_params=pltpu.CompilerParams(
            collective_id=0, has_side_effects=True, vmem_limit_bytes=48 * 1024 * 1024
        ),
        name="parareal",
    )(start_field, play_level, stiffness, columns, play_width, coil, newton_counts)
    return both[0], both[1]


def solution(mesh):
    return jax.shard_map(
        on_device,
        mesh=mesh,
        in_specs=(
            P("tm", None, "space"),
            P("tm", None, "space"),
            P(None, None, None, "space"),
            P(None, "space"),
            P(None, "space"),
            P(None, None, "space"),
            P("tm", None),
        ),
        out_specs=(P("tm", None, "space"), P("tm", None, "space")),
        check_vma=False,
    )
```
